128 devices in a mesh: tm: 8 (over y, core), tile: 16 (over x, z).
Axes of the slice: x: 4, y: 4, z: 4, core: 2. Of those that a mesh axis runs over, the one named last changes fastest.
Arguments:
- movie: bfloat16 [32, 1024, 1024], P('tm', 'tile'), may hold values from -6 to 6
- lift_weight: float32 [24], replicated, may hold values from -4 to 4
- lift_bias: float32 [24], replicated, may hold values from -3 to 3
- depth_kernel: float32 [3, 24, 9], replicated, may hold values from -2 to 2
- mix_weight: bfloat16 [3, 24, 24], replicated, may hold values from -1.25 to 1.25
- mix_bias: float32 [3, 24], replicated, may hold values from -3 to 3
- out_weight: float32 [24], replicated, may hold values from -1.25 to 1.25
- temporal_kernel: float32 [9], replicated, may hold values from -2 to 2
- footprints: bfloat16 [256, 1024, 1024], P(None, 'tile', 'tm'), may hold values from -0.0625 to 0.0625
- slot_owner: int32 [32768, 1], P(('tm', 'tile')), may hold values from 0 to 127; in each aligned block of 256 rows (0 to 255, 256 to 511, ...) at most 4 rows name the same one
- slot_neuron: int32 [32768], P(('tm', 'tile')), may hold values from 0 to 319
Outputs:
- filtered: bfloat16 [32, 1024, 1024], P(None, 'tile', 'tm')
- traces: float32 [40960, 32], P(('tm', 'tile'))
The draws below stay inside these ranges and needn't reach their ends.
Inputs may be any that keep to these rules, and one draw needn't show every extreme that they name: `slot_owner`: within the rows of one device (256 aligned rows), no owner is named more than 4 times.
All inputs are finite; a program needn't handle non-finite values.
Results may differ from the reference program's by a relative error of at most 0.012.
Values may be sent and summed in bfloat16 or wider, within the bound.
No kernel may reach another device: no remote copies, remote signals or barrier semaphores. Data moves between devices by JAX's collectives and lax.ppermute only.
A program may use at most 128 MiB of HBM per device.

```python
import math
import jax
import jax.numpy as jnp
import numpy as np
from jax import lax

C = 24
LAYERS = 3
KT = 9
ROWS_DEV = 64
COLS_DEV = 128
SLOTS_DEV = 256
NEUR_DEV = 320
FRAMES = 32
H = 1024
W = 1024
NEURONS = 40960
CAP = 4
N_TM = 8
N_TILE = 16


def with_ends(values, own_key, least, top_value):
    dims = values.shape
    place = [jax.random.randint(jax.random.fold_in(own_key, axis), (), 0, dims[axis]) for axis in range(len(dims))]
    values = values.at[tuple(place)].set(least)
    longest = dims.index(max(dims))
    place[longest] = (place[longest] + 1) % dims[longest]
    return values.at[tuple(place)].set(top_value)


def steps_of(own_key, dims, pieces, smallest, high):
    loudness, own = 1.0, jax.random.fold_in(own_key, 6)
    for dim, shards_of in pieces:
        heights = jnp.exp(jax.random.uniform(jax.random.fold_in(own, dim), (shards_of,), jnp.float32, smallest / len(pieces), high / len(pieces)))
        loudness = loudness * jnp.repeat(heights, dims[dim] // shards_of).reshape([-1 if axis == dim else 1 for axis in range(len(dims))])
    return loudness


def deal_out(own_key, own, number, rows, number_of, top, most, skew):
    order = jax.random.permutation(own_key, number_of)
    heavy_load, ordinary = portions_of(number_of, rows * top, most, skew, True), portions_of(number_of, rows * top, most, skew, False)
    places = jnp.arange(number_of)

    def named(tallies, turn):
        used = int((tallies > 0).sum())
        fixed = max(1, used // 4)
        moved = fixed + (places - fixed + turn * (used - fixed)) % max(1, number_of - fixed)
        return jnp.zeros((number_of,), jnp.int32).at[order[jnp.where(places < fixed, places, moved)]].set(jnp.asarray(tallies, jnp.int32))

    tallies = jnp.where(number % 4 == 0, named(heavy_load, number // 4), named(ordinary, number - number // 4 - 1))
    mixed = jax.random.permutation(jax.random.fold_in(own, 3), number_of)
    donor, receiver = mixed[0:number_of // 2 * 2:2], mixed[1:number_of // 2 * 2:2]
    room = jnp.minimum(tallies[donor] - 1, most - tallies[receiver]) // 2
    room = jnp.where((donor == order[0]) | (receiver == order[0]) | (tallies[receiver] == 0), 0, jnp.maximum(room, 0))
    moved = jax.random.randint(jax.random.fold_in(own, 4), (number_of // 2,), 0, 1 << 20) % (room + 1)
    tallies = tallies.at[donor].add(-moved).at[receiver].add(moved)
    members = jnp.searchsorted(jnp.cumsum(tallies), jnp.arange(rows * top), side="right").astype(jnp.int32)
    table = members.reshape(top, rows).T
    table = table[jax.random.permutation(jax.random.fold_in(own, 1), rows)]
    turn = jax.random.randint(jax.random.fold_in(own, 2), (rows, 1), 0, top)
    return jnp.take_along_axis(table, (jnp.arange(top)[None, :] + turn) % top, axis=1)


def portions_of(count, total, bound, lean, full):
    portions = [(1 << 20) // math.isqrt(grade ** lean) + 1 for grade in range(1, count + 1)]
    largest = bound if full else min(bound, max(-(-total // count), total * portions[0] // sum(portions)))
    least = 1 if total - largest >= count - 1 else 0
    holding, surplus = [largest] + [least] * (count - 1), total - largest - least * (count - 1)
    while surplus > 0:
        candidates = [i for i in range(1, count) if holding[i] < largest] or [i for i in range(1, count) if holding[i] < bound]
        mass, budget = sum([portions[i] for i in candidates]), surplus
        for i in candidates:
            addition = min(bound - holding[i], max(1, budget * portions[i] // mass), surplus)
            holding[i] = holding[i] + addition
            surplus = surplus - addition
    return np.array(holding)


def normal_values(rng, shape, width, reach, split=(), kind=jnp.bfloat16):
    factor_of = steps_of(rng, shape, split, -0.22, 0.18) if split else 1.0
    entries = jax.random.normal(rng, shape, jnp.float32) * width * factor_of
    return jnp.minimum(jnp.maximum(entries, -reach), reach).astype(kind)


def setup_inputs(seed: int = 0) -> dict:
    key_of = jax.random.split(jax.random.key(seed), 12)
    movie = normal_values(key_of[0], (FRAMES, H, W), 1.0, 6.0, ((0, 8), (1, 16)))
    lift_weight = normal_values(key_of[1], (C,), 1.0, 4.0, (), jnp.float32)
    lift_bias = normal_values(key_of[2], (C,), 0.5, 3.0, (), jnp.float32)
    depth_kernel = normal_values(key_of[3], (LAYERS, C, 9), 9 ** -0.5, 2.0, (), jnp.float32)
    mix_weight = normal_values(key_of[4], (LAYERS, C, C), C ** -0.5, 1.25)
    mix_bias = normal_values(key_of[5], (LAYERS, C), 0.5, 3.0, (), jnp.float32)
    out_weight = normal_values(key_of[6], (C,), C ** -0.5, 1.25, (), jnp.float32)
    temporal_kernel = normal_values(key_of[7], (KT,), KT ** -0.5, 2.0, (), jnp.float32)
    footprints = normal_values(key_of[8], (SLOTS_DEV, H, W), (ROWS_DEV * COLS_DEV) ** -0.5, 0.0625, ((1, 16), (2, 8)))
    slot_owner_keys = jax.random.split(jax.random.fold_in(key_of[9], 1), (N_TM * N_TILE * SLOTS_DEV) // SLOTS_DEV)
    slot_owner_turns = jax.random.permutation(jax.random.fold_in(key_of[9], 3), (N_TM * N_TILE * SLOTS_DEV) // SLOTS_DEV)
    slot_owner = jax.vmap(lambda own, number: deal_out(jax.random.fold_in(key_of[9], 2), own, number, SLOTS_DEV, N_TM * N_TILE, 1, CAP, 2))(slot_owner_keys, slot_owner_turns).reshape((N_TM * N_TILE * SLOTS_DEV, 1))
    slot_neuron = with_ends(jax.random.randint(key_of[10], (N_TM * N_TILE * SLOTS_DEV,), 0, NEUR_DEV), jax.random.fold_in(key_of[10], 1), 0, NEUR_DEV - 1).astype(jnp.int32)
    return dict(movie=movie, lift_weight=lift_weight, lift_bias=lift_bias, depth_kernel=depth_kernel, mix_weight=mix_weight, mix_bias=mix_bias, out_weight=out_weight, temporal_kernel=temporal_kernel, footprints=footprints, slot_owner=slot_owner, slot_neuron=slot_neuron)


def depthwise(features, kernel):
    row_count = features.shape[1]
    col_count = features.shape[2]
    padded = jnp.pad(features, ((0, 0), (1, 1), (1, 1)))
    summed = jnp.zeros(features.shape, jnp.float32)
    for row_shift in range(3):
        for col_shift in range(3):
            weight_tap = kernel[:, row_shift * 3 + col_shift][:, None, None]
            summed = summed + weight_tap * padded[:, row_shift:row_shift + row_count, col_shift:col_shift + col_count]
    return summed


def reference(movie, lift_weight, lift_bias, depth_kernel, mix_weight, mix_bias, out_weight, temporal_kernel, footprints, slot_owner, slot_neuron):
    def denoise_frame(frame):
        frame_f32 = frame.astype(jnp.float32)
        features = (lift_weight[:, None, None] * frame_f32[None] + lift_bias[:, None, None]).astype(jnp.bfloat16)
        for depth_step in range(LAYERS):
            spread = depthwise(features.astype(jnp.float32), depth_kernel[depth_step]).astype(jnp.bfloat16)
            mixed_sum = jnp.einsum("cd,chw->dhw", mix_weight[depth_step].astype(jnp.float32), spread.astype(jnp.float32), precision=lax.Precision.HIGHEST)
            mixed_sum = mixed_sum + mix_bias[depth_step][:, None, None]
            features = (features.astype(jnp.float32) + jnp.maximum(mixed_sum, 0.0)).astype(jnp.bfloat16)
        projected = jnp.sum(out_weight[:, None, None] * features.astype(jnp.float32), axis=0)
        return (frame_f32 + projected).astype(jnp.bfloat16)

    denoised = lax.map(denoise_frame, movie)
    half_taps = KT // 2
    padded = jnp.pad(denoised.astype(jnp.float32), ((half_taps, half_taps), (0, 0), (0, 0)))
    summed = jnp.zeros((FRAMES, H, W), jnp.float32)
    for tap_index in range(KT):
        summed = summed + temporal_kernel[tap_index] * padded[tap_index:tap_index + FRAMES]
    filtered = summed.astype(jnp.bfloat16)

    filtered_blocks = filtered.astype(jnp.float32).reshape(FRAMES, N_TILE, ROWS_DEV, N_TM, COLS_DEV)

    def slot_term(footprint):
        blocks = footprint.astype(jnp.float32).reshape(N_TILE, ROWS_DEV, N_TM, COLS_DEV)
        return jnp.einsum("jric,fjric->ijf", blocks, filtered_blocks, precision=lax.Precision.HIGHEST)

    partial_value = lax.map(slot_term, footprints)
    partial_value = jnp.transpose(partial_value, (1, 2, 0, 3)).reshape(N_TM * N_TILE * SLOTS_DEV, FRAMES)
    neuron_ids = (slot_owner[:, 0] * NEUR_DEV + slot_neuron).astype(jnp.int32)
    traces = jax.ops.segment_sum(partial_value, neuron_ids, num_segments=NEURONS)
    return filtered, traces
```

```python
import functools

import jax
import jax.numpy as jnp
from jax import lax
from jax.experimental import pallas as pl
from jax.experimental.pallas import tpu as pltpu
from jax.sharding import PartitionSpec as P

C = 24
LAYERS = 3
R = 64
HALO = LAYERS
RH = R + 2 * HALO
RP = 72
W = 1024
NT = 32
CAP = 4
NEUR_DEV = 320
ID_BASE = 32
BF = jnp.bfloat16
F32 = jnp.float32
VMEM = pl.BlockSpec(memory_space=pltpu.VMEM)
SMEM = pl.BlockSpec(memory_space=pltpu.SMEM)


def mix_matrices(depth_kernel, mix_weight, mix_bias):
    k = depth_kernel.reshape(LAYERS, C, 3, 3)
    w = jnp.einsum(
        "lcyx,lcd->lydcx", k, mix_weight.astype(F32), precision=lax.Precision.HIGHEST
    )
    j = jnp.arange(8)
    shift = j[None, :] - j[:, None] + 1
    main = jnp.zeros((LAYERS, 3, C, 8, C, 8), F32)
    for dx in range(3):
        main = main + w[:, :, :, None, :, None, dx] * (shift == dx).astype(F32)[:, None, :]
    main = main.reshape(LAYERS, 3, 192, 192)
    right = (w[..., 2][:, :, :, None, :] * (j == 7).astype(F32)[:, None]).reshape(LAYERS, 3, 192, C)
    left = (w[..., 0][:, :, :, None, :] * (j == 0).astype(F32)[:, None]).reshape(LAYERS, 3, 192, C)
    b = jnp.repeat(mix_bias, 8, axis=1)
    hi = b.astype(BF).astype(F32)
    bias = jnp.stack([hi, b - hi] + [jnp.zeros_like(b)] * 14, axis=-1)
    bias = bias[:, None] * (jnp.arange(3) == 1).astype(F32)[None, :, None, None]
    return jnp.concatenate([main, right, left, bias], axis=-1).astype(BF)


def denoise_kernel(*refs, NA, UN):
    def accs(rows, count):
        return [pltpu.ACC(p)((rows, 256), F32) for p in range(2) for _ in range(count)]

    pl.run_scoped(functools.partial(to_groups, *refs), *accs(2 * RP, 1))
    pl.run_scoped(
        lambda *acc: denoise_body(*refs, *acc, NA=NA, UN=UN),
        *accs(192, NA),
    )
    pl.run_scoped(functools.partial(from_groups, *refs), *accs(2 * R, 1))


def group_tile(n, k, transposed):
    cols = lax.broadcasted_iota(jnp.int32, (256, 256), int(transposed)) + 256 * k
    at = lax.broadcasted_iota(jnp.int32, (256, 256), 1 - int(transposed))
    return (cols == 8 * (at % 128) + 2 * n + at // 128).astype(F32).astype(BF)


def to_groups(edge_ref, mv_ref, w_ref, lw_ref, lb_ref, ow_ref, out_ref, x_ref, f_ref, m_ref, *accs):
    for n in range(4):
        for k in range(4):
            tile = group_tile(n, k, False)
            for p in range(2):
                pltpu.matmul_push_rhs(tile, 0, p)
            for p in range(2):
                pltpu.matmul_acc_lhs(
                    accs[p], mv_ref[p, :, k * 256 : (k + 1) * 256], load_staged_rhs=0
                )
        for p in range(2):
            got = pltpu.matmul_pop(accs[p])
            for h in range(2):
                for jj in range(2):
                    m_ref[p, h, pl.ds(2 * n + jj, RP, stride=8), :] = got[
                        h * RP : (h + 1) * RP, jj * 128 : (jj + 1) * 128
                    ]


def from_groups(edge_ref, mv_ref, w_ref, lw_ref, lb_ref, ow_ref, out_ref, x_ref, f_ref, m_ref, *accs):
    def rows(p, n):
        parts = [
            [m_ref[p, h, pl.ds(8 * HALO + 2 * n + jj, R, stride=8), :] for jj in range(2)]
            for h in range(2)
        ]
        return jnp.concatenate([jnp.concatenate(q, axis=1) for q in parts], axis=0).astype(BF)

    for k in range(4):
        for n in range(4):
            tile = group_tile(n, k, True)
            for p in range(2):
                pltpu.matmul_push_rhs(tile, 0, p)
            for p in range(2):
                pltpu.matmul_acc_lhs(accs[p], rows(p, n), load_staged_rhs=0)
        for p in range(2):
            got = pltpu.matmul_pop(accs[p]).astype(BF)
            for h in range(2):
                for q in range(2):
                    out_ref[2 * k + q, 2 * p + h] = got[
                        h * R : (h + 1) * R, q * 128 : (q + 1) * 128
                    ]


def denoise_body(
    edge_ref, mv_ref, w_ref, lw_ref, lb_ref, ow_ref, out_ref, x_ref, f_ref, m_ref, *accs, NA, UN
):
    accs = (accs[:NA], accs[NA:])
    lanes = lax.broadcasted_iota(jnp.int32, (C, 128), 1)
    first = lanes == 0
    last = lanes == 127
    ones = (lax.broadcasted_iota(jnp.int32, (16, 256), 0) < 2).astype(F32).astype(BF)

    def movie_row(p, y):
        at = pl.multiple_of(y * 8, 8)
        return jnp.concatenate([m_ref[p, h, pl.ds(at, 8), :] for h in range(2)], axis=1)

    def put(p, y, new, slot):
        x_ref[p, y, 0:192, :] = new.astype(BF)
        for h in range(2):
            f_ref[slot, h] = new[:, h * 128 : (h + 1) * 128]
        right = []
        left = []
        for h in range(2):
            r0 = f_ref[slot, h, pl.ds(0, C, stride=8), :]
            l7 = f_ref[slot, h, pl.ds(7, C, stride=8), :]
            right.append(jnp.where(last, 0.0, pltpu.roll(r0, 127, 1)))
            left.append(jnp.where(first, 0.0, pltpu.roll(l7, 1, 1)))
        halo = jnp.concatenate([jnp.concatenate(right, 1), jnp.concatenate(left, 1)], 0)
        x_ref[p, y, 192:240, :] = halo.astype(BF)

    def lift_row(y, _):
        for p in range(2):
            m = movie_row(p, y)
            x_ref[p, y, 240:256, :] = ones
            put(p, y, jnp.concatenate([m * lw_ref[c] + lb_ref[c] for c in range(C)], axis=0), p)
        return 0

    lax.fori_loop(0, RH, lift_row, 0)

    def zero_edges():
        for side, rows in ((0, range(HALO)), (1, range(RH - HALO, RH))):

            @pl.when(edge_ref[side] == 1)
            def _():
                for p in range(2):
                    for y in rows:
                        x_ref[p, y, 0:240, :] = jnp.zeros((240, 256), BF)

    zero_edges()

    for layer in range(LAYERS):
        lo, hi = layer + 1, RH - layer - 1

        def tile(y, terms):
            for p in range(2):
                pltpu.matmul_push_rhs(x_ref[p, y], 0, p)
            for n, (dy, a) in enumerate(terms):
                for p in range(2):
                    pltpu.matmul_acc_lhs(
                        accs[p][a % NA], w_ref[layer, dy], load_staged_rhs=0 if n == 0 else None
                    )

        def finish(y, a, slot):
            for p in range(2):
                mixed = pltpu.matmul_pop(accs[p][a % NA])
                new = x_ref[p, y, 0:192, :].astype(F32) + jnp.maximum(mixed, 0.0)
                if layer < LAYERS - 1:
                    put(p, y, new, slot * 2 + p)
                else:
                    new = new.astype(BF).astype(F32)
                    total = new[0:8] * ow_ref[0]
                    for c in range(1, C):
                        total = total + new[8 * c : 8 * c + 8] * ow_ref[c]
                    total = movie_row(p, y) + total
                    for h in range(2):
                        at = pl.multiple_of(y * 8, 8)
                        m_ref[p, h, pl.ds(at, 8), :] = total[:, h * 128 : (h + 1) * 128]

        def step(y, i):
            tile(y, [(2, i - 1), (1, i), (0, i + 1)])
            finish(y - 1, i - 1, i % 2)

        tile(lo - 1, [(0, 0)])
        tile(lo, [(0, 1), (1, 0)])
        n_main = hi - lo - 2

        def body(b, _):
            for u in range(UN):
                step(lo + 1 + b * UN + u, 1 + u)
            return 0

        n_loop = n_main // UN
        lax.fori_loop(0, n_loop, body, 0)
        for u in range(n_main - n_loop * UN):
            step(lo + 1 + n_loop * UN + u, 1 + u)
        i = n_main + 1
        tile(hi - 1, [(2, i - 1), (1, i)])
        finish(hi - 2, i - 1, 0)
        tile(hi, [(2, i)])
        finish(hi - 1, i, 1)
        if layer < LAYERS - 1:
            zero_edges()


def denoise(edge, movie, mats, lift_weight, lift_bias, out_weight, NA=4, UN=8):
    return pl.pallas_call(
        functools.partial(denoise_kernel, NA=NA, UN=UN),
        out_shape=jax.ShapeDtypeStruct((8, 4, R, 128), BF),
        in_specs=[SMEM, VMEM, VMEM, SMEM, SMEM, SMEM],
        out_specs=VMEM,
        scratch_shapes=[
            pltpu.VMEM((2, RH, 256, 256), BF),
            pltpu.VMEM((4, 2, 192, 128), F32),
            pltpu.VMEM((2, 2, RP * 8, 128), F32),
        ],
        compiler_params=pltpu.CompilerParams(vmem_limit_bytes=56 * 2**20),
        name="denoise",
    )(edge, movie, mats, lift_weight, lift_bias, out_weight)


def gather_kernel(got_ref, out_ref):
    got = got_ref[...].astype(F32)
    ids = got[:, NT : NT + 1] * ID_BASE + got[:, NT + 1 : NT + 2]
    n_of = lax.broadcasted_iota(jnp.int32, (got.shape[0], NEUR_DEV), 1)
    hot = (n_of == ids.astype(jnp.int32)).astype(F32).astype(BF)
    out_ref[...] = lax.dot_general(
        hot, got_ref[:, :NT], (((0,), (0,)), ((), ())), preferred_element_type=F32
    )


def gather(got):
    return pl.pallas_call(
        gather_kernel,
        out_shape=jax.ShapeDtypeStruct((NEUR_DEV, NT), F32),
        in_specs=[VMEM],
        out_specs=VMEM,
        name="gather",
    )(got)


def temporal(received, temporal_kernel):
    frame_count = received.shape[0]
    tap_count = temporal_kernel.shape[0]
    half_taps = tap_count // 2
    padded = jnp.pad(received.astype(F32), ((half_taps, half_taps), (0, 0), (0, 0)))
    summed = jnp.zeros(received.shape, F32)
    for tap_index in range(tap_count):
        summed = summed + temporal_kernel[tap_index] * padded[tap_index : tap_index + frame_count]
    return summed.astype(BF)


def local(
    movie,
    lift_weight,
    lift_bias,
    depth_kernel,
    mix_weight,
    mix_bias,
    out_weight,
    temporal_kernel,
    footprints,
    slot_owner,
    slot_neuron,
):
    n_tile = lax.axis_size("tile")
    me = lax.axis_index("tile")
    up = [(i, i + 1) for i in range(n_tile - 1)]
    down = [(b, a) for a, b in up]
    low = lax.ppermute(movie[:, R - HALO :], "tile", up)
    high = lax.ppermute(movie[:, :HALO], "tile", down)
    pad = jnp.zeros((4, RP - RH, W), BF)
    widened = jnp.concatenate([low, movie, high, pad], axis=1)
    edge = jnp.stack([me == 0, me == n_tile - 1]).astype(jnp.int32)
    mats = mix_matrices(depth_kernel, mix_weight, mix_bias)
    denoised = denoise(edge, widened.reshape(2, 2 * RP, W), mats, lift_weight, lift_bias, out_weight)
    received = lax.all_to_all(denoised, "tm", 0, 0, tiled=True)
    filtered = temporal(received.reshape(NT, R, 128), temporal_kernel)
    slots = footprints.shape[0]
    partial = lax.dot_general(
        footprints.reshape(slots, R * 128),
        filtered.reshape(NT, R * 128),
        (((1,), (1,)), ((), ())),
        preferred_element_type=F32,
    )
    owner = slot_owner[:, 0]
    s = jnp.arange(slots)
    earlier = (owner[:, None] == owner[None, :]) & (s[None, :] < s[:, None])
    position = owner * CAP + jnp.sum(earlier, axis=1, dtype=jnp.int32)
    n_dev = lax.axis_size("tm") * n_tile
    hot = (jnp.arange(n_dev * CAP)[:, None] == position[None, :]).astype(BF)
    ids = jnp.stack([slot_neuron // ID_BASE, slot_neuron % ID_BASE], axis=1).astype(BF)
    sending = jnp.concatenate([partial.astype(BF), ids], axis=1)
    outgoing = lax.dot(hot, sending, preferred_element_type=F32).astype(BF)
    arriving = lax.all_to_all(
        outgoing.reshape(n_dev, CAP, NT + 2), ("tm", "tile"), 0, 0, tiled=True
    )
    return filtered, gather(arriving.reshape(n_dev * CAP, NT + 2))


def solution(mesh):
    return jax.shard_map(
        local,
        mesh=mesh,
        in_specs=(
            P("tm", "tile", None),
            P(),
            P(),
            P(),
            P(),
            P(),
            P(),
            P(),
            P(None, "tile", "tm"),
            P(("tm", "tile"), None),
            P(("tm", "tile")),
        ),
        out_specs=(P(None, "tile", "tm"), P(("tm", "tile"), None)),
        check_vma=False,
    )
```

```python
import functools

import jax
import jax.numpy as jnp
from jax import lax
from jax.experimental import pallas as pl
from jax.experimental.pallas import tpu as pltpu
from jax.sharding import PartitionSpec as P

C = 24
LAYERS = 3
R = 64
HALO = LAYERS
RH = R + 2 * HALO
W = 1024
NT = 32
CAP = 4
NEUR_DEV = 320
ID_BASE = 32
BF = jnp.bfloat16
F32 = jnp.float32
VMEM = pl.BlockSpec(memory_space=pltpu.VMEM)
SMEM = pl.BlockSpec(memory_space=pltpu.SMEM)


def mix_kernel(dk_ref, mix_ref, bias_ref, out_ref):
    col = lax.broadcasted_iota(jnp.int32, (C, 256), 1)
    chan = lax.broadcasted_iota(jnp.int32, (C, 256), 0)
    right = (col >= 192) & (col < 216)
    left = (col >= 216) & (col < 240)
    c_of = jnp.where(right, col - 192, jnp.where(left, col - 216, col // 8))
    spread = ((c_of == chan) & (col < 240)).astype(F32)
    j_in = lax.broadcasted_iota(jnp.int32, (8, 256), 1)
    j_out = lax.broadcasted_iota(jnp.int32, (8, 256), 0)
    right = (j_in >= 192) & (j_in < 216)
    left = (j_in >= 216) & (j_in < 240)
    dx_of = jnp.where(right, 8, jnp.where(left, -1, j_in % 8)) - j_out + 1
    row = lax.broadcasted_iota(jnp.int32, (C, C), 0)
    eye = row == lax.broadcasted_iota(jnp.int32, (C, C), 1)
    over_rows = (((0,), (0,)), ((), ()))
    for layer in range(LAYERS):
        mixed = lax.dot_general(
            mix_ref[layer].astype(F32), spread, over_rows, precision=lax.Precision.HIGHEST
        )
        taps = lax.dot_general(
            dk_ref[layer], spread, over_rows, precision=lax.Precision.HIGHEST
        )
        bias = jnp.sum(jnp.where(eye, bias_ref[layer : layer + 1, :], 0.0), axis=1, keepdims=True)
        high = bias.astype(BF).astype(F32)
        bias = jnp.where(col == 240, high, jnp.where(col == 241, bias - high, 0.0))
        for dy in range(3):
            tap = jnp.zeros((8, 256), F32)
            for dx in range(3):
                tap = tap + jnp.where(dx_of == dx, taps[3 * dy + dx : 3 * dy + dx + 1, :], 0.0)
            for d in range(0, C, 2):
                both = [
                    mixed[e : e + 1, :] * tap + (bias[e : e + 1, :] if dy == 1 else 0.0)
                    for e in (d, d + 1)
                ]
                out_ref[layer, dy, 8 * d : 8 * d + 16, :] = jnp.concatenate(both, 0).astype(BF)


def mix_matrices(depth_kernel, mix_weight, mix_bias):
    return pl.pallas_call(
        mix_kernel,
        out_shape=jax.ShapeDtypeStruct((LAYERS, 3, 192, 256), BF),
        in_specs=[VMEM, VMEM, VMEM],
        out_specs=VMEM,
        cost_estimate=pl.CostEstimate(flops=20_000_000, bytes_accessed=1_000_000, transcendentals=0),
        name="mix_matrices",
    )(depth_kernel, mix_weight, mix_bias)


def denoise_kernel(*refs, NA, UN):
    def accs(rows, count):
        return [pltpu.ACC(p)((rows, 256), F32) for p in range(2) for _ in range(count)]

    pl.run_scoped(functools.partial(to_groups, *refs), *accs(2 * R + 16, 1))
    pl.run_scoped(
        lambda *acc: denoise_body(*refs, *acc, NA=NA, UN=UN),
        *accs(192, NA),
    )
    pl.run_scoped(functools.partial(from_groups, *refs), *accs(2 * R, 1))


def group_tile(n, k, transposed):
    cols = lax.broadcasted_iota(jnp.int32, (256, 256), int(transposed)) + 256 * k
    at = lax.broadcasted_iota(jnp.int32, (256, 256), 1 - int(transposed))
    return (cols == 8 * (at % 128) + 2 * n + at // 128).astype(F32).astype(BF)


def to_groups(edge_ref, mv_ref, halo_ref, w_ref, lw_ref, lb_ref, ow_ref, out_ref, x_ref, f_ref, m_ref, *accs):
    for n in range(4):
        for k in range(4):
            tile = group_tile(n, k, False)
            for p in range(2):
                pltpu.matmul_push_rhs(tile, 0, p)
            for p in range(2):
                at = slice(k * 256, (k + 1) * 256)
                rows = jnp.concatenate([mv_ref[p, :, at], halo_ref[p, :, at]], axis=0)
                pltpu.matmul_acc_lhs(accs[p], rows, load_staged_rhs=0)
        for p in range(2):
            got = pltpu.matmul_pop(accs[p])
            for h in range(2):
                for jj in range(2):
                    cut = got[:, jj * 128 : (jj + 1) * 128]
                    j = 2 * n + jj
                    top = 2 * R + 2 * HALO * h
                    m_ref[p, h, pl.ds(8 * HALO + j, R, stride=8), :] = cut[h * R : (h + 1) * R]
                    m_ref[p, h, pl.ds(j, HALO, stride=8), :] = cut[top : top + HALO]
                    m_ref[p, h, pl.ds(8 * (HALO + R) + j, HALO, stride=8), :] = cut[
                        top + HALO : top + 2 * HALO
                    ]


def from_groups(edge_ref, mv_ref, halo_ref, w_ref, lw_ref, lb_ref, ow_ref, out_ref, x_ref, f_ref, m_ref, *accs):
    def rows(p, n):
        parts = [
            [m_ref[p, h, pl.ds(8 * HALO + 2 * n + jj, R, stride=8), :] for jj in range(2)]
            for h in range(2)
        ]
        return jnp.concatenate([jnp.concatenate(q, axis=1) for q in parts], axis=0).astype(BF)

    for k in range(4):
        for n in range(4):
            tile = group_tile(n, k, True)
            for p in range(2):
                pltpu.matmul_push_rhs(tile, 0, p)
            for p in range(2):
                pltpu.matmul_acc_lhs(accs[p], rows(p, n), load_staged_rhs=0)
        for p in range(2):
            got = pltpu.matmul_pop(accs[p]).astype(BF)
            for h in range(2):
                for q in range(2):
                    out_ref[2 * k + q, 2 * p + h] = got[
                        h * R : (h + 1) * R, q * 128 : (q + 1) * 128
                    ]


def denoise_body(
    edge_ref, mv_ref, halo_ref, w_ref, lw_ref, lb_ref, ow_ref, out_ref, x_ref, f_ref, m_ref, *accs, NA, UN
):
    accs = (accs[:NA], accs[NA:])
    lanes = lax.broadcasted_iota(jnp.int32, (C, 128), 1)
    first = lanes == 0
    last = lanes == 127
    ones = (lax.broadcasted_iota(jnp.int32, (16, 256), 0) < 2).astype(F32).astype(BF)

    def movie_row(p, y):
        at = pl.multiple_of(y * 8, 8)
        return jnp.concatenate([m_ref[p, h, pl.ds(at, 8), :] for h in range(2)], axis=1)

    def put(p, y, new, slot):
        x_ref[p, y, 0:192, :] = new.astype(BF)
        for h in range(2):
            f_ref[slot, h] = new[:, h * 128 : (h + 1) * 128]
        right = []
        left = []
        for h in range(2):
            r0 = f_ref[slot, h, pl.ds(0, C, stride=8), :]
            l7 = f_ref[slot, h, pl.ds(7, C, stride=8), :]
            right.append(jnp.where(last, 0.0, pltpu.roll(r0, 127, 1)))
            left.append(jnp.where(first, 0.0, pltpu.roll(l7, 1, 1)))
        halo = jnp.concatenate([jnp.concatenate(right, 1), jnp.concatenate(left, 1)], 0)
        x_ref[p, y, 192:240, :] = halo.astype(BF)

    def lift_row(y, _):
        for p in range(2):
            m = movie_row(p, y)
            x_ref[p, y, 240:256, :] = ones
            put(p, y, jnp.concatenate([m * lw_ref[c] + lb_ref[c] for c in range(C)], axis=0), p)
        return 0

    lax.fori_loop(0, RH, lift_row, 0)

    def zero_edges():
        for side, rows in ((0, range(HALO)), (1, range(RH - HALO, RH))):

            @pl.when(edge_ref[side] == 1)
            def _():
                for p in range(2):
                    for y in rows:
                        x_ref[p, y, 0:240, :] = jnp.zeros((240, 256), BF)

    zero_edges()

    for layer in range(LAYERS):
        lo, hi = layer + 1, RH - layer - 1

        def tile(y, terms):
            for p in range(2):
                pltpu.matmul_push_rhs(x_ref[p, y], 0, p)
            for n, (dy, a) in enumerate(terms):
                for p in range(2):
                    pltpu.matmul_acc_lhs(
                        accs[p][a % NA], w_ref[layer, dy], load_staged_rhs=0 if n == 0 else None
                    )

        def finish(y, a, slot):
            for p in range(2):
                mixed = pltpu.matmul_pop(accs[p][a % NA])
                new = x_ref[p, y, 0:192, :].astype(F32) + jnp.maximum(mixed, 0.0)
                if layer < LAYERS - 1:
                    put(p, y, new, slot * 2 + p)
                else:
                    new = new.astype(BF).astype(F32)
                    total = new[0:8] * ow_ref[0]
                    for c in range(1, C):
                        total = total + new[8 * c : 8 * c + 8] * ow_ref[c]
                    total = movie_row(p, y) + total
                    for h in range(2):
                        at = pl.multiple_of(y * 8, 8)
                        m_ref[p, h, pl.ds(at, 8), :] = total[:, h * 128 : (h + 1) * 128]

        def step(y, i):
            tile(y, [(2, i - 1), (1, i), (0, i + 1)])
            finish(y - 1, i - 1, i % 2)

        tile(lo - 1, [(0, 0)])
        tile(lo, [(0, 1), (1, 0)])
        n_main = hi - lo - 2

        def body(b, _):
            for u in range(UN):
                step(lo + 1 + b * UN + u, 1 + u)
            return 0

        n_loop = n_main // UN
        lax.fori_loop(0, n_loop, body, 0)
        for u in range(n_main - n_loop * UN):
            step(lo + 1 + n_loop * UN + u, 1 + u)
        i = n_main + 1
        tile(hi - 1, [(2, i - 1), (1, i)])
        finish(hi - 2, i - 1, 0)
        tile(hi, [(2, i)])
        finish(hi - 1, i, 1)
        if layer < LAYERS - 1:
            zero_edges()


def denoise(edge, movie, halo, mats, lift_weight, lift_bias, out_weight, NA=4, UN=8):
    return pl.pallas_call(
        functools.partial(denoise_kernel, NA=NA, UN=UN),
        out_shape=jax.ShapeDtypeStruct((8, 4, R, 128), BF),
        in_specs=[SMEM, VMEM, VMEM, VMEM, SMEM, SMEM, SMEM],
        out_specs=VMEM,
        scratch_shapes=[
            pltpu.VMEM((2, RH, 256, 256), BF),
            pltpu.VMEM((4, 2, 192, 128), F32),
            pltpu.VMEM((2, 2, RH * 8, 128), F32),
        ],
        compiler_params=pltpu.CompilerParams(vmem_limit_bytes=56 * 2**20),
        name="denoise",
    )(edge, movie, halo, mats, lift_weight, lift_bias, out_weight)


def relay_kernel(foot_ref, own_row_ref, own_col_ref, id_ref, after_ref, out_ref, hot_ref, ids_ref, s_ref):
    slots = foot_ref.shape[0]
    own_row = own_row_ref[...]
    own_col = own_col_ref[...]
    before = lax.broadcasted_iota(jnp.int32, (slots, slots), 0) < lax.broadcasted_iota(
        jnp.int32, (slots, slots), 1
    )
    rank = jnp.sum(((own_row == own_col) & before).astype(jnp.int32), axis=0, keepdims=True)
    place = own_row * CAP + rank
    hot = place == lax.broadcasted_iota(jnp.int32, hot_ref.shape, 0)
    hot_ref[...] = hot.astype(F32).astype(BF)
    ids = id_ref[...]
    second = lax.broadcasted_iota(jnp.int32, (slots, 2), 1) == 1
    ids_ref[...] = jnp.where(second, ids % ID_BASE, ids // ID_BASE).astype(F32).astype(BF)

    def part(g, _):
        r0 = pl.multiple_of(g * 16, 16)

        def slot(b, _):
            for u in range(16):
                s = b * 16 + u
                s_ref[pl.ds(s, 16, stride=slots), :] = foot_ref[s, pl.ds(r0, 16), :].astype(F32)
            return 0

        lax.fori_loop(0, slots // 16, slot, 0)
        for q in range(8):
            two = [s_ref[(2 * q + e) * slots : (2 * q + e + 1) * slots, :] for e in range(2)]
            out_ref[g * 8 + q] = jnp.concatenate(two, axis=1).astype(BF)
        return 0

    lax.fori_loop(0, R // 16, part, 0)


def relay(footprints, slot_owner, slot_neuron, n_dev, after):
    slots = footprints.shape[0]
    return pl.pallas_call(
        relay_kernel,
        out_shape=(
            jax.ShapeDtypeStruct((R // 2, slots, 256), BF),
            jax.ShapeDtypeStruct((n_dev * CAP, slots), BF),
            jax.ShapeDtypeStruct((slots, 2), BF),
        ),
        in_specs=[VMEM] * 4 + [pl.BlockSpec(memory_space=pl.ANY)],
        out_specs=(VMEM, VMEM, VMEM),
        scratch_shapes=[pltpu.VMEM((16 * slots, 128), F32)],
        compiler_params=pltpu.CompilerParams(vmem_limit_bytes=24 * 2**20),
        cost_estimate=pl.CostEstimate(flops=20_000_000, bytes_accessed=12_000_000, transcendentals=0),
        name="relay",
    )(footprints, slot_owner.reshape(1, slots), slot_owner, slot_neuron.reshape(slots, 1), after)


def trace_kernel(got_ref, tk_ref, foot_ref, hot_ref, ids_ref, filt_ref, send_ref, g_ref):
    half = 4
    for r0 in range(0, R, 16):
        frames = [got_ref[t, r0 : r0 + 16, :].astype(F32) for t in range(NT)]
        for t in range(NT):
            total = None
            for k in range(2 * half + 1):
                u = t + k - half
                if 0 <= u < NT:
                    term = tk_ref[k] * frames[u]
                    total = term if total is None else total + term
            out = total.astype(BF)
            filt_ref[t, r0 : r0 + 16, :] = out
            g_ref[pl.ds(r0 * NT + t, 16, stride=NT), :] = out.astype(F32)
    total = jnp.zeros((foot_ref.shape[1], NT), F32)
    for q in range(R // 2):
        two = [g_ref[(2 * q + e) * NT : (2 * q + e + 1) * NT, :] for e in range(2)]
        rows = jnp.concatenate(two, axis=1).astype(BF)
        total = total + lax.dot_general(
            foot_ref[q], rows, (((1,), (1,)), ((), ())), preferred_element_type=F32
        )
    sending = jnp.concatenate([total.astype(BF).astype(F32), ids_ref[...].astype(F32)], axis=1)
    send_ref[...] = jnp.dot(
        hot_ref[...], sending.astype(BF), preferred_element_type=F32
    ).astype(BF)


def trace(received, temporal_kernel, foot, hot, ids):
    return pl.pallas_call(
        trace_kernel,
        out_shape=(
            jax.ShapeDtypeStruct((NT, R, 128), BF),
            jax.ShapeDtypeStruct((hot.shape[0], NT + 2), BF),
        ),
        in_specs=[VMEM, SMEM, VMEM, VMEM, VMEM],
        out_specs=(VMEM, VMEM),
        scratch_shapes=[pltpu.VMEM((R * NT, 128), F32)],
        compiler_params=pltpu.CompilerParams(vmem_limit_bytes=24 * 2**20),
        name="trace",
    )(received, temporal_kernel, foot, hot, ids)


def gather_kernel(got_ref, out_ref):
    got = got_ref[...].astype(F32)
    ids = got[:, NT : NT + 1] * ID_BASE + got[:, NT + 1 : NT + 2]
    n_of = lax.broadcasted_iota(jnp.int32, (got.shape[0], NEUR_DEV), 1)
    hot = (n_of == ids.astype(jnp.int32)).astype(F32).astype(BF)
    out_ref[...] = lax.dot_general(
        got_ref[:, :NT], hot, (((0,), (0,)), ((), ())), preferred_element_type=F32
    )


def gather(got):
    return pl.pallas_call(
        gather_kernel,
        out_shape=jax.ShapeDtypeStruct((NT, NEUR_DEV), F32),
        in_specs=[VMEM],
        out_specs=VMEM,
        name="gather",
    )(got).T


def local(
    movie,
    lift_weight,
    lift_bias,
    depth_kernel,
    mix_weight,
    mix_bias,
    out_weight,
    temporal_kernel,
    footprints,
    slot_owner,
    slot_neuron,
):
    n_tile = lax.axis_size("tile")
    me = lax.axis_index("tile")
    up = [(i, i + 1) for i in range(n_tile - 1)]
    down = [(b, a) for a, b in up]
    low = lax.ppermute(movie[:, R - HALO :], "tile", up)
    high = lax.ppermute(movie[:, :HALO], "tile", down)
    halo = jnp.concatenate([low, high], axis=1).reshape(2, 4 * HALO, W)
    halo = jnp.pad(halo, ((0, 0), (0, 16 - 4 * HALO), (0, 0)))
    edge = jnp.stack([me == 0, me == n_tile - 1]).astype(jnp.int32)
    mats = mix_matrices(depth_kernel, mix_weight, mix_bias)
    denoised = denoise(
        edge, movie.reshape(2, 2 * R, W), halo, mats, lift_weight, lift_bias, out_weight
    )
    n_dev = lax.axis_size("tm") * n_tile
    received = lax.all_to_all(denoised, "tm", 0, 0, tiled=True)
    foot, hot, ids = relay(footprints, slot_owner, slot_neuron, n_dev, denoised)
    filtered, outgoing = trace(received.reshape(NT, R, 128), temporal_kernel, foot, hot, ids)
    arriving = lax.all_to_all(
        outgoing.reshape(n_dev, CAP, NT + 2), ("tm", "tile"), 0, 0, tiled=True
    )
    return filtered, gather(arriving.reshape(n_dev * CAP, NT + 2))


def solution(mesh):
    return jax.shard_map(
        local,
        mesh=mesh,
        in_specs=(
            P("tm", "tile", None),
            P(),
            P(),
            P(),
            P(),
            P(),
            P(),
            P(),
            P(None, "tile", "tm"),
            P(("tm", "tile"), None),
            P(("tm", "tile")),
        ),
        out_specs=(P(None, "tile", "tm"), P(("tm", "tile"), None)),
        check_vma=False,
    )
```

```python
import functools

import jax
import jax.numpy as jnp
from jax import lax
from jax.experimental import pallas as pl
from jax.experimental.pallas import tpu as pltpu
from jax.sharding import PartitionSpec as P

C = 24
LAYERS = 3
R = 64
HALO = LAYERS
RH = R + 2 * HALO
RP = 72
STEP = 14
W = 1024
NT = 32
CAP = 4
NEUR_DEV = 320
ID_BASE = 32
BF = jnp.bfloat16
F32 = jnp.float32
VMEM = pl.BlockSpec(memory_space=pltpu.VMEM)
HBM = pl.BlockSpec(memory_space=pltpu.HBM)
SMEM = pl.BlockSpec(memory_space=pltpu.SMEM)


def mix_kernel(dk_ref, mix_ref, bias_ref, lw_ref, lb_ref, out_ref, lift_ref, b_ref):
    col = lax.broadcasted_iota(jnp.int32, (C, 256), 1)
    chan = lax.broadcasted_iota(jnp.int32, (C, 256), 0)
    right = (col >= 192) & (col < 216)
    left = (col >= 216) & (col < 240)
    c_of = jnp.where(right, col - 192, jnp.where(left, col - 216, col // 8))
    spread = ((c_of == chan) & (col < 240)).astype(F32)
    j_in = lax.broadcasted_iota(jnp.int32, (8, 256), 1)
    j_out = lax.broadcasted_iota(jnp.int32, (8, 256), 0)
    right = (j_in >= 192) & (j_in < 216)
    left = (j_in >= 216) & (j_in < 240)
    dx_of = jnp.where(right, 8, jnp.where(left, -1, j_in % 8)) - j_out + 1
    row = lax.broadcasted_iota(jnp.int32, (C, C), 0)
    eye = row == lax.broadcasted_iota(jnp.int32, (C, C), 1)
    over_rows = (((0,), (0,)), ((), ()))
    for layer in range(1, LAYERS):
        mixed = lax.dot_general(
            mix_ref[layer].astype(F32), spread, over_rows, precision=lax.Precision.HIGHEST
        )
        taps = jnp.dot(dk_ref[:, layer, :], spread, precision=lax.Precision.HIGHEST)
        bias = jnp.sum(jnp.where(eye, bias_ref[layer : layer + 1, :], 0.0), axis=1, keepdims=True)
        high = bias.astype(BF).astype(F32)
        bias = jnp.where(col == 240, high, jnp.where(col == 241, bias - high, 0.0))
        for dy in range(3):
            tap = jnp.zeros((8, 256), F32)
            for dx in range(3):
                tap = tap + jnp.where(dx_of == dx, taps[3 * dy + dx : 3 * dy + dx + 1, :], 0.0)
            for d in range(0, C, 2):
                both = [
                    mixed[e : e + 1, :] * tap + (bias[e : e + 1, :] if dy == 1 else 0.0)
                    for e in (d, d + 1)
                ]
                out_ref[layer - 1, dy, 8 * d : 8 * d + 16, :] = jnp.concatenate(both, 0).astype(BF)

    def column(row_value):
        return jnp.sum(jnp.where(eye, row_value, 0.0), axis=1, keepdims=True)

    first = mix_ref[0].astype(F32)
    by_weight, by_bias = (
        lax.dot_general(
            first,
            dk_ref[:, 0, :] * ref[...],
            (((0,), (1,)), ((), ())),
            precision=lax.Precision.HIGHEST,
        )
        for ref in (lw_ref, lb_ref)
    )
    bias = column(bias_ref[0:1, :]) + jnp.sum(by_bias, axis=1, keepdims=True)
    high = bias.astype(BF).astype(F32)
    bias = jnp.where(col == 29, high, jnp.where(col == 30, bias - high, 0.0))
    highs = [v.astype(BF).astype(F32) for v in (by_weight, by_bias)]
    split = jnp.concatenate(
        [highs[0], by_weight - highs[0], highs[1], by_bias - highs[1]], axis=1
    ).astype(BF)
    tap = lax.broadcasted_iota(jnp.int32, (9, 256), 0)
    at = lax.broadcasted_iota(jnp.int32, (9, 256), 1)
    same = at // 16 == tap // 3
    dx = tap % 3
    place = at % 16
    for j in range(8):
        to = j + dx - 1
        to = jnp.where(to == 8, 8, jnp.where(to == -1, 9, to))
        pick = (same & (place == to)).astype(F32)
        off = place == 12
        if j == 7:
            off = off | ((place == 10) & (dx == 2))
        if j == 0:
            off = off | ((place == 11) & (dx == 0))
        drop = jnp.where(same & off, -1.0, 0.0)
        picks = jnp.concatenate([pick, pick, drop, drop], axis=0).astype(BF)
        value = bias + jnp.dot(split, picks, preferred_element_type=F32)
        for h in range(2):
            b_ref[h, pl.ds(j, C, stride=8), :] = value[:, h * 128 : (h + 1) * 128]
    block = jnp.concatenate([b_ref[0], b_ref[1]], axis=1)
    for r in range(STEP):
        lift_ref[r] = (pltpu.roll(block, 16 * r, 1) if r else block).astype(BF)


def mix_matrices(depth_kernel, mix_weight, mix_bias, lift_weight, lift_bias):
    return pl.pallas_call(
        mix_kernel,
        out_shape=(
            jax.ShapeDtypeStruct((LAYERS - 1, 3, 192, 256), BF),
            jax.ShapeDtypeStruct((STEP, 192, 256), BF),
        ),
        in_specs=[VMEM] * 5,
        out_specs=(VMEM, VMEM),
        scratch_shapes=[pltpu.VMEM((2, 192, 128), F32)],
        cost_estimate=pl.CostEstimate(flops=20_000_000, bytes_accessed=1_000_000, transcendentals=0),
        name="mix_matrices",
    )(depth_kernel.transpose(2, 0, 1), mix_weight, mix_bias, lift_weight.reshape(1, C), lift_bias.reshape(1, C))


def denoise_kernel(*refs, NA, UN):
    def accs(rows, count):
        return [pltpu.ACC(p)((rows, 256), F32) for p in range(2) for _ in range(count)]

    pl.run_scoped(functools.partial(to_groups, *refs), *accs(2 * R + 16, 1))
    pl.run_scoped(
        lambda *acc: denoise_body(*refs, *acc, NA=NA, UN=UN),
        *accs(192, NA),
    )
    pl.run_scoped(functools.partial(from_groups, *refs), *accs(2 * R, 1))


def group_tile(n, k, transposed):
    cols = lax.broadcasted_iota(jnp.int32, (256, 256), int(transposed)) + 256 * k
    at = lax.broadcasted_iota(jnp.int32, (256, 256), 1 - int(transposed))
    return (cols == 8 * (at % 128) + 2 * n + at // 128).astype(F32).astype(BF)


def to_groups(edge_ref, mv_ref, halo_ref, w_ref, w0_ref, lw_ref, lb_ref, ow_ref, out_ref, after_ref, x_ref, f_ref, m_ref, t_ref, *accs):
    for n in range(4):
        for k in range(4):
            tile = group_tile(n, k, False)
            for p in range(2):
                pltpu.matmul_push_rhs(tile, 0, p)
            for p in range(2):
                at = slice(k * 256, (k + 1) * 256)
                rows = jnp.concatenate([mv_ref[p, :, at], halo_ref[p, :, at]], axis=0)
                pltpu.matmul_acc_lhs(accs[p], rows, load_staged_rhs=0)
        for p in range(2):
            got = pltpu.matmul_pop(accs[p])
            for h in range(2):
                for jj in range(2):
                    cut = got[:, jj * 128 : (jj + 1) * 128]
                    j = 2 * n + jj
                    top = 2 * R + 2 * HALO * h
                    m_ref[p, h, pl.ds(8 * HALO + j, R, stride=8), :] = cut[h * R : (h + 1) * R]
                    m_ref[p, h, pl.ds(j, HALO, stride=8), :] = cut[top : top + HALO]
                    m_ref[p, h, pl.ds(8 * (HALO + R) + j, HALO, stride=8), :] = cut[
                        top + HALO : top + 2 * HALO
                    ]


def from_groups(edge_ref, mv_ref, halo_ref, w_ref, w0_ref, lw_ref, lb_ref, ow_ref, out_ref, after_ref, x_ref, f_ref, m_ref, t_ref, *accs):
    def rows(p, n):
        parts = [
            [m_ref[p, h, pl.ds(8 * HALO + 2 * n + jj, R, stride=8), :] for jj in range(2)]
            for h in range(2)
        ]
        return jnp.concatenate([jnp.concatenate(q, axis=1) for q in parts], axis=0).astype(BF)

    for k in range(4):
        for n in range(4):
            tile = group_tile(n, k, True)
            for p in range(2):
                pltpu.matmul_push_rhs(tile, 0, p)
            for p in range(2):
                pltpu.matmul_acc_lhs(accs[p], rows(p, n), load_staged_rhs=0)
        for p in range(2):
            got = pltpu.matmul_pop(accs[p]).astype(BF)
            for h in range(2):
                for q in range(2):
                    out_ref[2 * k + q, 2 * p + h] = got[
                        h * R : (h + 1) * R, q * 128 : (q + 1) * 128
                    ]


def denoise_body(
    edge_ref, mv_ref, halo_ref, w_ref, w0_ref, lw_ref, lb_ref, ow_ref, out_ref, after_ref, x_ref, f_ref, m_ref, t_ref, *accs, NA, UN
):
    accs = (accs[:NA], accs[NA:])
    lanes = lax.broadcasted_iota(jnp.int32, (C, 128), 1)
    first = lanes == 0
    last = lanes == 127
    ones = (lax.broadcasted_iota(jnp.int32, (16, 256), 0) < 2).astype(F32).astype(BF)

    def movie_row(p, y):
        at = pl.multiple_of(y * 8, 8)
        return jnp.concatenate([m_ref[p, h, pl.ds(at, 8), :] for h in range(2)], axis=1)

    def put(p, y, new, slot):
        x_ref[p, y, 0:192, :] = new.astype(BF)
        for h in range(2):
            f_ref[slot, h] = new[:, h * 128 : (h + 1) * 128]
        right = []
        left = []
        for h in range(2):
            r0 = f_ref[slot, h, pl.ds(0, C, stride=8), :]
            l7 = f_ref[slot, h, pl.ds(7, C, stride=8), :]
            right.append(jnp.where(last, 0.0, pltpu.roll(r0, 127, 1)))
            left.append(jnp.where(first, 0.0, pltpu.roll(l7, 1, 1)))
        halo = jnp.concatenate([jnp.concatenate(right, 1), jnp.concatenate(left, 1)], 0)
        x_ref[p, y, 192:240, :] = halo.astype(BF)

    sub = lax.broadcasted_iota(jnp.int32, (8, 128), 0)
    lane = lax.broadcasted_iota(jnp.int32, (8, 128), 1)
    bias_rows = (sub == 5) | (sub == 6)
    rest = bias_rows | ((sub == 2) & (lane == 127)) | ((sub == 3) & (lane == 0))
    rest = rest.astype(F32)
    for p in range(2):
        for h in range(2):
            m_ref[p, h, 8 * RH :, :] = jnp.zeros((8 * (RP - RH), 128), F32)

    def frame_row(y, _):
        for p in range(2):
            parts = []
            for h in range(2):
                m = m_ref[p, h, pl.ds(pl.multiple_of(y * 8, 8), 8), :]
                right = jnp.where((sub == 0) & (lane < 127), pltpu.roll(m, 127, 1), 0.0)
                left = pltpu.roll(pltpu.roll(m, 1, 1), 2, 0)
                left = jnp.where((sub == 1) & (lane > 0), left, 0.0)
                parts.append(jnp.concatenate([m, right + left + rest], axis=0))
            at = pl.multiple_of(y * 16, 16)
            t_ref[p, pl.ds(at, 16), :] = jnp.concatenate(parts, axis=1).astype(BF)
        return 0

    lax.fori_loop(0, RP, frame_row, 0, unroll=4)
    off_row = (lax.broadcasted_iota(jnp.int32, (16, 256), 0) == 12).astype(F32).astype(BF)

    def at_edges(store):
        for side, rows in ((0, range(HALO)), (1, range(RH - HALO, RH))):

            @pl.when(edge_ref[side] == 1)
            def _():
                for p in range(2):
                    for y in rows:
                        store(p, y)

    def off_frame(p, y):
        t_ref[p, 16 * y : 16 * y + 16, :] = off_row

    def off_features(p, y):
        x_ref[p, y, 0:240, :] = jnp.zeros((240, 256), BF)

    at_edges(off_frame)

    def first_layer(b, _):
        y0 = b * STEP
        for p in range(2):
            rows = t_ref[p, pl.ds(pl.multiple_of(y0 * 16, 16), 256), :]
            pltpu.matmul_push_rhs(rows, 0, p)

        def issue(r):
            for p in range(2):
                pltpu.matmul_acc_lhs(
                    accs[p][r % NA], w0_ref[r], load_staged_rhs=0 if r == 0 else None
                )

        def done(r):
            y = y0 + r + 1
            for p in range(2):
                mixed = pltpu.matmul_pop(accs[p][r % NA])
                m = movie_row(p, y)
                new = [
                    m * lw_ref[c] + lb_ref[c] + jnp.maximum(mixed[8 * c : 8 * c + 8], 0.0)
                    for c in range(C)
                ]
                x_ref[p, y, 240:256, :] = ones
                put(p, y, jnp.concatenate(new, axis=0), (r % 2) * 2 + p)

        issue(0)
        for r in range(1, STEP):
            issue(r)
            done(r - 1)
        done(STEP - 1)
        return 0

    for p in range(2):
        x_ref[p, 0, 240:256, :] = ones
    lax.fori_loop(0, (RH + STEP - 3) // STEP, first_layer, 0)
    at_edges(off_features)

    for layer in range(1, LAYERS):
        lo, hi = layer + 1, RH - layer - 1

        def push(y, a):
            for p in range(2):
                pltpu.matmul_push_rhs(x_ref[p, y], a % 2, p)

        def tile(i, terms):
            for n, (dy, a) in enumerate(terms):
                for p in range(2):
                    pltpu.matmul_acc_lhs(
                        accs[p][a % NA],
                        w_ref[layer - 1, dy],
                        load_staged_rhs=i % 2 if n == 0 else None,
                    )

        def finish(y, a, slot):
            for p in range(2):
                mixed = pltpu.matmul_pop(accs[p][a % NA])
                new = x_ref[p, y, 0:192, :].astype(F32) + jnp.maximum(mixed, 0.0)
                if layer < LAYERS - 1:
                    put(p, y, new, slot * 2 + p)
                else:
                    new = new.astype(BF).astype(F32)
                    total = new[0:8] * ow_ref[0]
                    for c in range(1, C):
                        total = total + new[8 * c : 8 * c + 8] * ow_ref[c]
                    total = movie_row(p, y) + total
                    for h in range(2):
                        at = pl.multiple_of(y * 8, 8)
                        m_ref[p, h, pl.ds(at, 8), :] = total[:, h * 128 : (h + 1) * 128]

        def step(y, i):
            push(y + 1, i + 1)
            tile(i, [(2, i - 1), (1, i), (0, i + 1)])
            finish(y - 1, i - 1, i % 2)

        push(lo - 1, 1)
        push(lo, 0)
        tile(1, [(0, 0)])
        push(lo + 1, 1)
        tile(0, [(0, 1), (1, 0)])
        n_main = hi - lo - 2

        def body(b, _):
            for u in range(UN):
                step(lo + 1 + b * UN + u, 1 + u)
            return 0

        n_loop = n_main // UN
        lax.fori_loop(0, n_loop, body, 0)
        for u in range(n_main - n_loop * UN):
            step(lo + 1 + n_loop * UN + u, 1 + u)
        i = n_main + 1
        push(hi, i + 1)
        tile(i, [(2, i - 1), (1, i)])
        finish(hi - 2, i - 1, 0)
        tile(i + 1, [(2, i)])
        finish(hi - 1, i, 1)
        if layer < LAYERS - 1:
            at_edges(off_features)

    after_ref[...] = jnp.zeros(after_ref.shape, F32)


def denoise(edge, movie, halo, mats, lift_mats, lift_weight, lift_bias, out_weight, NA=4, UN=8):
    return pl.pallas_call(
        functools.partial(denoise_kernel, NA=NA, UN=UN),
        out_shape=(
            jax.ShapeDtypeStruct((8, 4, R, 128), BF),
            jax.ShapeDtypeStruct((8, 128), F32),
        ),
        in_specs=[SMEM, VMEM, VMEM, VMEM, VMEM, SMEM, SMEM, SMEM],
        out_specs=(VMEM, VMEM),
        scratch_shapes=[
            pltpu.VMEM((2, RP, 256, 256), BF),
            pltpu.VMEM((4, 2, 192, 128), F32),
            pltpu.VMEM((2, 2, RP * 8, 128), F32),
            pltpu.VMEM((2, RP * 16, 256), BF),
        ],
        compiler_params=pltpu.CompilerParams(vmem_limit_bytes=56 * 2**20),
        name="denoise",
    )(edge, movie, halo, mats, lift_mats, lift_weight, lift_bias, out_weight)


def relay_kernel(foot_any, after_ref, out_any, in_ref, s_ref, o_ref, in_sem, out_sem):
    slots = foot_any.shape[0]
    parts = R // 16
    pitch = slots + 8

    def load(g):
        return pltpu.make_async_copy(
            foot_any.at[:, pl.ds(16 * g, 16), :], in_ref.at[g % 2], in_sem.at[g % 2]
        )

    def save(g):
        return pltpu.make_async_copy(
            o_ref.at[g % 2], out_any.at[pl.ds(8 * g, 8)], out_sem.at[g % 2]
        )

    load(0).start()

    for g in range(parts):
        if g + 1 < parts:
            load(g + 1).start()
        load(g).wait()

        def slot(b, _):
            for u in range(16):
                s = b * 16 + u
                s_ref[pl.ds(s, 16, stride=pitch), :] = in_ref[g % 2, s].astype(F32)
            return 0

        lax.fori_loop(0, slots // 16, slot, 0)
        if g >= 2:
            save(g - 2).wait()
        for q in range(8):
            two = [s_ref[(2 * q + e) * pitch : (2 * q + e) * pitch + slots, :] for e in range(2)]
            o_ref[g % 2, q] = jnp.concatenate(two, axis=1).astype(BF)
        save(g).start()
    for g in range(parts - 2, parts):
        save(g).wait()


def relay(footprints, after):
    slots = footprints.shape[0]
    return pl.pallas_call(
        relay_kernel,
        out_shape=jax.ShapeDtypeStruct((R // 2, slots, 256), BF),
        in_specs=[HBM, VMEM],
        out_specs=HBM,
        scratch_shapes=[
            pltpu.VMEM((2, slots, 16, 128), BF),
            pltpu.VMEM((16 * (slots + 8), 128), F32),
            pltpu.VMEM((2, 8, slots, 256), BF),
            pltpu.SemaphoreType.DMA((2,)),
            pltpu.SemaphoreType.DMA((2,)),
        ],
        compiler_params=pltpu.CompilerParams(vmem_limit_bytes=61 * 2**20),
        cost_estimate=pl.CostEstimate(flops=20_000_000, bytes_accessed=12_000_000, transcendentals=0),
        name="relay",
    )(footprints, after)


def trace_kernel(
    got_ref, tk_ref, foot_any, own_ref, id_ref, filt_ref, send_ref, g_ref, foot_ref, sem
):
    half = 4
    pitch = NT + 8
    parts = R // 16
    copies = [
        pltpu.make_async_copy(
            foot_any.at[pl.ds(8 * g, 8)], foot_ref.at[pl.ds(8 * g, 8)], sem.at[g]
        )
        for g in range(parts)
    ]
    for copy in copies:
        copy.start()
    traces = jnp.zeros((foot_ref.shape[1], NT), F32)
    for g in range(parts):
        r0 = 16 * g
        frames = [got_ref[t, r0 : r0 + 16, :].astype(F32) for t in range(NT)]
        for t in range(NT):
            total = None
            for k in range(2 * half + 1):
                u = t + k - half
                if 0 <= u < NT:
                    term = tk_ref[k] * frames[u]
                    total = term if total is None else total + term
            out = total.astype(BF)
            filt_ref[t, r0 : r0 + 16, :] = out
            g_ref[pl.ds(t, 16, stride=pitch), :] = out.astype(F32)
        copies[g].wait()
        for q in range(8):
            two = [g_ref[(2 * q + e) * pitch : (2 * q + e) * pitch + NT, :] for e in range(2)]
            rows = jnp.concatenate(two, axis=1).astype(BF)
            traces = traces + lax.dot_general(
                foot_ref[8 * g + q], rows, (((1,), (1,)), ((), ())), preferred_element_type=F32
            )
    slots = foot_any.shape[1]
    own_row = own_ref[...]
    r_of = lax.broadcasted_iota(jnp.int32, (slots, slots), 0)
    c_of = lax.broadcasted_iota(jnp.int32, (slots, slots), 1)

    def column(row):
        picked = jnp.where(r_of == c_of, row.astype(F32), 0.0)
        return jnp.sum(picked, axis=1, keepdims=True).astype(jnp.int32)

    own_col = column(own_row)
    rank = jnp.where((own_row == own_col) & (r_of < c_of), 1.0, 0.0)
    rank = jnp.sum(rank, axis=0, keepdims=True).astype(jnp.int32)
    place = own_row * CAP + rank
    hot = place == lax.broadcasted_iota(jnp.int32, (send_ref.shape[0], slots), 0)
    hot = hot.astype(F32).astype(BF)
    ids = column(id_ref[...])
    second = lax.broadcasted_iota(jnp.int32, (slots, 2), 1) == 1
    ids = jnp.where(second, ids % ID_BASE, ids // ID_BASE).astype(F32)
    sending = jnp.concatenate([traces, ids], axis=1)
    send_ref[...] = jnp.dot(
        hot, sending.astype(BF), preferred_element_type=F32
    ).astype(BF)


def trace(received, temporal_kernel, foot, slot_owner, slot_neuron, n_dev):
    slots = foot.shape[1]
    return pl.pallas_call(
        trace_kernel,
        out_shape=(
            jax.ShapeDtypeStruct((NT, R, 128), BF),
            jax.ShapeDtypeStruct((n_dev * CAP, NT + 2), BF),
        ),
        in_specs=[VMEM, SMEM, HBM, VMEM, VMEM],
        out_specs=(VMEM, VMEM),
        scratch_shapes=[
            pltpu.VMEM((16 * (NT + 8), 128), F32),
            pltpu.VMEM(foot.shape, BF),
            pltpu.SemaphoreType.DMA((R // 16,)),
        ],
        compiler_params=pltpu.CompilerParams(vmem_limit_bytes=50 * 2**20),
        name="trace",
    )(received, temporal_kernel, foot, slot_owner.reshape(1, slots), slot_neuron.reshape(1, slots))


def gather_kernel(got_ref, out_ref):
    got = got_ref[...].astype(F32)
    ids = got[:, NT : NT + 1] * ID_BASE + got[:, NT + 1 : NT + 2]
    n_of = lax.broadcasted_iota(jnp.int32, (got.shape[0], NEUR_DEV), 1)
    hot = (n_of == ids.astype(jnp.int32)).astype(F32).astype(BF)
    out_ref[...] = lax.dot_general(
        got_ref[:, :NT], hot, (((0,), (0,)), ((), ())), preferred_element_type=F32
    )


def gather(got):
    return pl.pallas_call(
        gather_kernel,
        out_shape=jax.ShapeDtypeStruct((NT, NEUR_DEV), F32),
        in_specs=[VMEM],
        out_specs=VMEM,
        name="gather",
    )(got).T


def local(
    movie,
    lift_weight,
    lift_bias,
    depth_kernel,
    mix_weight,
    mix_bias,
    out_weight,
    temporal_kernel,
    footprints,
    slot_owner,
    slot_neuron,
):
    n_tile = lax.axis_size("tile")
    me = lax.axis_index("tile")
    up = [(i, i + 1) for i in range(n_tile - 1)]
    down = [(b, a) for a, b in up]
    low = lax.ppermute(movie[:, R - HALO :], "tile", up)
    high = lax.ppermute(movie[:, :HALO], "tile", down)
    halo = jnp.concatenate([low, high], axis=1).reshape(2, 4 * HALO, W)
    halo = jnp.pad(halo, ((0, 0), (0, 16 - 4 * HALO), (0, 0)))
    edge = jnp.stack([me == 0, me == n_tile - 1]).astype(jnp.int32)
    mats, lift_mats = mix_matrices(depth_kernel, mix_weight, mix_bias, lift_weight, lift_bias)
    denoised, after = denoise(
        edge, movie.reshape(2, 2 * R, W), halo, mats, lift_mats, lift_weight, lift_bias, out_weight
    )
    n_dev = lax.axis_size("tm") * n_tile
    received = lax.all_to_all(denoised, "tm", 0, 0, tiled=True)
    foot = relay(footprints, after)
    filtered, outgoing = trace(
        received.reshape(NT, R, 128), temporal_kernel, foot, slot_owner, slot_neuron, n_dev
    )
    arriving = lax.all_to_all(
        outgoing.reshape(n_dev, CAP, NT + 2), ("tm", "tile"), 0, 0, tiled=True
    )
    return filtered, gather(arriving.reshape(n_dev * CAP, NT + 2))


def solution(mesh):
    return jax.shard_map(
        local,
        mesh=mesh,
        in_specs=(
            P("tm", "tile", None),
            P(),
            P(),
            P(),
            P(),
            P(),
            P(),
            P(),
            P(None, "tile", "tm"),
            P(("tm", "tile"), None),
            P(("tm", "tile")),
        ),
        out_specs=(P(None, "tile", "tm"), P(("tm", "tile"), None)),
        check_vma=False,
    )
```

```python
import functools

import jax
import jax.numpy as jnp
from jax import lax
from jax.experimental import pallas as pl
from jax.experimental.pallas import tpu as pltpu
from jax.sharding import PartitionSpec as P

C = 24
LAYERS = 3
R = 64
HALO = LAYERS
RH = R + 2 * HALO
RP = 72
STEP = 14
W = 1024
NT = 32
CAP = 4
NEUR_DEV = 320
ID_BASE = 32
BF = jnp.bfloat16
F32 = jnp.float32
VMEM = pl.BlockSpec(memory_space=pltpu.VMEM)
HBM = pl.BlockSpec(memory_space=pltpu.HBM)
SMEM = pl.BlockSpec(memory_space=pltpu.SMEM)


def mix_kernel(dk_ref, mix_ref, bias_ref, lw_ref, lb_ref, out_ref, lift_ref, b_ref):
    col = lax.broadcasted_iota(jnp.int32, (C, 256), 1)
    chan = lax.broadcasted_iota(jnp.int32, (C, 256), 0)
    right = (col >= 192) & (col < 216)
    left = (col >= 216) & (col < 240)
    c_of = jnp.where(right, col - 192, jnp.where(left, col - 216, col // 8))
    spread = ((c_of == chan) & (col < 240)).astype(F32)
    j_in = lax.broadcasted_iota(jnp.int32, (8, 256), 1)
    j_out = lax.broadcasted_iota(jnp.int32, (8, 256), 0)
    right = (j_in >= 192) & (j_in < 216)
    left = (j_in >= 216) & (j_in < 240)
    dx_of = jnp.where(right, 8, jnp.where(left, -1, j_in % 8)) - j_out + 1
    row = lax.broadcasted_iota(jnp.int32, (C, C), 0)
    eye = row == lax.broadcasted_iota(jnp.int32, (C, C), 1)
    over_rows = (((0,), (0,)), ((), ()))
    for layer in range(1, LAYERS):
        mixed = lax.dot_general(
            mix_ref[layer].astype(F32), spread, over_rows, precision=lax.Precision.HIGHEST
        )
        taps = jnp.dot(dk_ref[:, layer, :], spread, precision=lax.Precision.HIGHEST)
        bias = jnp.sum(jnp.where(eye, bias_ref[layer : layer + 1, :], 0.0), axis=1, keepdims=True)
        high = bias.astype(BF).astype(F32)
        bias = jnp.where(col == 240, high, jnp.where(col == 241, bias - high, 0.0))
        for dy in range(3):
            tap = jnp.zeros((8, 256), F32)
            for dx in range(3):
                tap = tap + jnp.where(dx_of == dx, taps[3 * dy + dx : 3 * dy + dx + 1, :], 0.0)
            for d in range(0, C, 2):
                both = [
                    mixed[e : e + 1, :] * tap + (bias[e : e + 1, :] if dy == 1 else 0.0)
                    for e in (d, d + 1)
                ]
                out_ref[layer - 1, dy, 8 * d : 8 * d + 16, :] = jnp.concatenate(both, 0).astype(BF)

    def column(row_value):
        return jnp.sum(jnp.where(eye, row_value, 0.0), axis=1, keepdims=True)

    first = mix_ref[0].astype(F32)
    by_weight, by_bias = (
        lax.dot_general(
            first,
            dk_ref[:, 0, :] * ref[...],
            (((0,), (1,)), ((), ())),
            precision=lax.Precision.HIGHEST,
        )
        for ref in (lw_ref, lb_ref)
    )
    bias = column(bias_ref[0:1, :]) + jnp.sum(by_bias, axis=1, keepdims=True)
    high = bias.astype(BF).astype(F32)
    bias = jnp.where(col == 29, high, jnp.where(col == 30, bias - high, 0.0))
    highs = [v.astype(BF).astype(F32) for v in (by_weight, by_bias)]
    split = jnp.concatenate(
        [highs[0], by_weight - highs[0], highs[1], by_bias - highs[1]], axis=1
    ).astype(BF)
    tap = lax.broadcasted_iota(jnp.int32, (9, 256), 0)
    at = lax.broadcasted_iota(jnp.int32, (9, 256), 1)
    same = at // 16 == tap // 3
    dx = tap % 3
    place = at % 16
    for j in range(8):
        to = j + dx - 1
        to = jnp.where(to == 8, 8, jnp.where(to == -1, 9, to))
        pick = (same & (place == to)).astype(F32)
        off = place == 12
        if j == 7:
            off = off | ((place == 10) & (dx == 2))
        if j == 0:
            off = off | ((place == 11) & (dx == 0))
        drop = jnp.where(same & off, -1.0, 0.0)
        picks = jnp.concatenate([pick, pick, drop, drop], axis=0).astype(BF)
        value = bias + jnp.dot(split, picks, preferred_element_type=F32)
        for h in range(2):
            b_ref[h, pl.ds(j, C, stride=8), :] = value[:, h * 128 : (h + 1) * 128]
    block = jnp.concatenate([b_ref[0], b_ref[1]], axis=1)
    for r in range(STEP):
        lift_ref[r] = (pltpu.roll(block, 16 * r, 1) if r else block).astype(BF)


def mix_matrices(depth_kernel, mix_weight, mix_bias, lift_weight, lift_bias):
    return pl.pallas_call(
        mix_kernel,
        out_shape=(
            jax.ShapeDtypeStruct((LAYERS - 1, 3, 192, 256), BF),
            jax.ShapeDtypeStruct((STEP, 192, 256), BF),
        ),
        in_specs=[VMEM] * 5,
        out_specs=(VMEM, VMEM),
        scratch_shapes=[pltpu.VMEM((2, 192, 128), F32)],
        cost_estimate=pl.CostEstimate(flops=20_000_000, bytes_accessed=1_000_000, transcendentals=0),
        name="mix_matrices",
    )(depth_kernel.transpose(2, 0, 1), mix_weight, mix_bias, lift_weight.reshape(1, C), lift_bias.reshape(1, C))


def denoise_kernel(*refs, NA, UN):
    def accs(rows, count):
        return [pltpu.ACC(p)((rows, 256), F32) for p in range(2) for _ in range(count)]

    pl.run_scoped(functools.partial(to_groups, *refs), *accs(2 * R + 16, 1))
    pl.run_scoped(
        lambda *acc: denoise_body(*refs, *acc, NA=NA, UN=UN),
        *accs(192, NA),
    )
    pl.run_scoped(functools.partial(from_groups, *refs), *accs(2 * R, 1))


def group_tile(n, k, transposed):
    cols = lax.broadcasted_iota(jnp.int32, (256, 256), int(transposed)) + 256 * k
    at = lax.broadcasted_iota(jnp.int32, (256, 256), 1 - int(transposed))
    return (cols == 8 * (at % 128) + 2 * n + at // 128).astype(F32).astype(BF)


def to_groups(edge_ref, mv_ref, halo_ref, w_ref, w0_ref, lw_ref, lb_ref, ow_ref, out_ref, after_ref, x_ref, f_ref, m_ref, t_ref, *accs):
    for n in range(4):
        for k in range(4):
            tile = group_tile(n, k, False)
            for p in range(2):
                pltpu.matmul_push_rhs(tile, 0, p)
            for p in range(2):
                at = slice(k * 256, (k + 1) * 256)
                rows = jnp.concatenate([mv_ref[p, :, at], halo_ref[p, :, at]], axis=0)
                pltpu.matmul_acc_lhs(accs[p], rows, load_staged_rhs=0)
        for p in range(2):
            got = pltpu.matmul_pop(accs[p])
            for h in range(2):
                for jj in range(2):
                    cut = got[:, jj * 128 : (jj + 1) * 128]
                    j = 2 * n + jj
                    top = 2 * R + 2 * HALO * h
                    m_ref[p, h, pl.ds(8 * HALO + j, R, stride=8), :] = cut[h * R : (h + 1) * R]
                    m_ref[p, h, pl.ds(j, HALO, stride=8), :] = cut[top : top + HALO]
                    m_ref[p, h, pl.ds(8 * (HALO + R) + j, HALO, stride=8), :] = cut[
                        top + HALO : top + 2 * HALO
                    ]


def from_groups(edge_ref, mv_ref, halo_ref, w_ref, w0_ref, lw_ref, lb_ref, ow_ref, out_ref, after_ref, x_ref, f_ref, m_ref, t_ref, *accs):
    def rows(p, n):
        parts = [
            [m_ref[p, h, pl.ds(8 * HALO + 2 * n + jj, R, stride=8), :] for jj in range(2)]
            for h in range(2)
        ]
        return jnp.concatenate([jnp.concatenate(q, axis=1) for q in parts], axis=0).astype(BF)

    for k in range(4):
        for n in range(4):
            tile = group_tile(n, k, True)
            for p in range(2):
                pltpu.matmul_push_rhs(tile, 0, p)
            for p in range(2):
                pltpu.matmul_acc_lhs(accs[p], rows(p, n), load_staged_rhs=0)
        for p in range(2):
            got = pltpu.matmul_pop(accs[p]).astype(BF)
            for h in range(2):
                for q in range(2):
                    out_ref[2 * k + q, 2 * p + h] = got[
                        h * R : (h + 1) * R, q * 128 : (q + 1) * 128
                    ]


def denoise_body(
    edge_ref, mv_ref, halo_ref, w_ref, w0_ref, lw_ref, lb_ref, ow_ref, out_ref, after_ref, x_ref, f_ref, m_ref, t_ref, *accs, NA, UN
):
    accs = (accs[:NA], accs[NA:])
    lanes = lax.broadcasted_iota(jnp.int32, (C, 128), 1)
    first = lanes == 0
    last = lanes == 127
    ones = (lax.broadcasted_iota(jnp.int32, (16, 256), 0) < 2).astype(F32).astype(BF)

    def movie_row(p, y):
        at = pl.multiple_of(y * 8, 8)
        return jnp.concatenate([m_ref[p, h, pl.ds(at, 8), :] for h in range(2)], axis=1)

    def put(p, y, new, slot):
        x_ref[p, y, 0:192, :] = new.astype(BF)
        for h in range(2):
            f_ref[slot, h] = new[:, h * 128 : (h + 1) * 128]
        right = []
        left = []
        for h in range(2):
            r0 = f_ref[slot, h, pl.ds(0, C, stride=8), :]
            l7 = f_ref[slot, h, pl.ds(7, C, stride=8), :]
            right.append(jnp.where(last, 0.0, pltpu.roll(r0, 127, 1)))
            left.append(jnp.where(first, 0.0, pltpu.roll(l7, 1, 1)))
        halo = jnp.concatenate([jnp.concatenate(right, 1), jnp.concatenate(left, 1)], 0)
        x_ref[p, y, 192:240, :] = halo.astype(BF)

    sub = lax.broadcasted_iota(jnp.int32, (8, 128), 0)
    lane = lax.broadcasted_iota(jnp.int32, (8, 128), 1)
    bias_rows = (sub == 5) | (sub == 6)
    rest = bias_rows | ((sub == 2) & (lane == 127)) | ((sub == 3) & (lane == 0))
    rest = rest.astype(F32)
    for p in range(2):
        for h in range(2):
            m_ref[p, h, 8 * RH :, :] = jnp.zeros((8 * (RP - RH), 128), F32)

    def frame_row(y, _):
        for p in range(2):
            parts = []
            for h in range(2):
                m = m_ref[p, h, pl.ds(pl.multiple_of(y * 8, 8), 8), :]
                right = jnp.where((sub == 0) & (lane < 127), pltpu.roll(m, 127, 1), 0.0)
                left = pltpu.roll(pltpu.roll(m, 1, 1), 2, 0)
                left = jnp.where((sub == 1) & (lane > 0), left, 0.0)
                parts.append(jnp.concatenate([m, right + left + rest], axis=0))
            at = pl.multiple_of(y * 16, 16)
            t_ref[p, pl.ds(at, 16), :] = jnp.concatenate(parts, axis=1).astype(BF)
        return 0

    lax.fori_loop(0, RP, frame_row, 0, unroll=4)
    off_row = (lax.broadcasted_iota(jnp.int32, (16, 256), 0) == 12).astype(F32).astype(BF)

    def at_edges(store):
        for side, rows in ((0, range(HALO)), (1, range(RH - HALO, RH))):

            @pl.when(edge_ref[side] == 1)
            def _():
                for p in range(2):
                    for y in rows:
                        store(p, y)

    def off_frame(p, y):
        t_ref[p, 16 * y : 16 * y + 16, :] = off_row

    def off_features(p, y):
        x_ref[p, y, 0:240, :] = jnp.zeros((240, 256), BF)

    at_edges(off_frame)

    def first_layer(b, _):
        y0 = b * STEP
        for p in range(2):
            rows = t_ref[p, pl.ds(pl.multiple_of(y0 * 16, 16), 256), :]
            pltpu.matmul_push_rhs(rows, 0, p)

        def issue(r):
            for p in range(2):
                pltpu.matmul_acc_lhs(
                    accs[p][r % NA], w0_ref[r], load_staged_rhs=0 if r == 0 else None
                )

        def done(r):
            y = y0 + r + 1
            for p in range(2):
                mixed = pltpu.matmul_pop(accs[p][r % NA])
                m = movie_row(p, y)
                new = [
                    m * lw_ref[c] + lb_ref[c] + jnp.maximum(mixed[8 * c : 8 * c + 8], 0.0)
                    for c in range(C)
                ]
                x_ref[p, y, 240:256, :] = ones
                put(p, y, jnp.concatenate(new, axis=0), (r % 2) * 2 + p)

        issue(0)
        for r in range(1, STEP):
            issue(r)
            done(r - 1)
        done(STEP - 1)
        return 0

    for p in range(2):
        x_ref[p, 0, 240:256, :] = ones
    lax.fori_loop(0, (RH + STEP - 3) // STEP, first_layer, 0)
    at_edges(off_features)

    for layer in range(1, LAYERS):
        lo, hi = layer + 1, RH - layer - 1

        def push(y, a):
            for p in range(2):
                pltpu.matmul_push_rhs(x_ref[p, y], a % 2, p)

        def tile(i, terms):
            for n, (dy, a) in enumerate(terms):
                for p in range(2):
                    pltpu.matmul_acc_lhs(
                        accs[p][a % NA],
                        w_ref[layer - 1, dy],
                        load_staged_rhs=i % 2 if n == 0 else None,
                    )

        def finish(y, a, slot):
            for p in range(2):
                mixed = pltpu.matmul_pop(accs[p][a % NA])
                new = x_ref[p, y, 0:192, :].astype(F32) + jnp.maximum(mixed, 0.0)
                if layer < LAYERS - 1:
                    put(p, y, new, slot * 2 + p)
                else:
                    new = new.astype(BF).astype(F32)
                    total = new[0:8] * ow_ref[0]
                    for c in range(1, C):
                        total = total + new[8 * c : 8 * c + 8] * ow_ref[c]
                    total = movie_row(p, y) + total
                    for h in range(2):
                        at = pl.multiple_of(y * 8, 8)
                        m_ref[p, h, pl.ds(at, 8), :] = total[:, h * 128 : (h + 1) * 128]

        def step(y, i):
            push(y + 1, i + 1)
            tile(i, [(2, i - 1), (1, i), (0, i + 1)])
            finish(y - 1, i - 1, i % 2)

        push(lo - 1, 1)
        push(lo, 0)
        tile(1, [(0, 0)])
        push(lo + 1, 1)
        tile(0, [(0, 1), (1, 0)])
        n_main = hi - lo - 2
        un = UN[layer - 1]

        def body(b, _):
            for u in range(un):
                step(lo + 1 + b * un + u, 1 + u)
            return 0

        n_loop = n_main // un
        lax.fori_loop(0, n_loop, body, 0)
        for u in range(n_main - n_loop * un):
            step(lo + 1 + n_loop * un + u, 1 + u)
        i = n_main + 1
        push(hi, i + 1)
        tile(i, [(2, i - 1), (1, i)])
        finish(hi - 2, i - 1, 0)
        tile(i + 1, [(2, i)])
        finish(hi - 1, i, 1)
        if layer < LAYERS - 1:
            at_edges(off_features)

    after_ref[...] = jnp.zeros(after_ref.shape, F32)


def denoise(edge, movie, halo, mats, lift_mats, lift_weight, lift_bias, out_weight, NA=4, UN=(16, 20)):
    return pl.pallas_call(
        functools.partial(denoise_kernel, NA=NA, UN=UN),
        out_shape=(
            jax.ShapeDtypeStruct((8, 4, R, 128), BF),
            jax.ShapeDtypeStruct((8, 128), F32),
        ),
        in_specs=[SMEM, VMEM, VMEM, VMEM, VMEM, SMEM, SMEM, SMEM],
        out_specs=(VMEM, VMEM),
        scratch_shapes=[
            pltpu.VMEM((2, RP, 256, 256), BF),
            pltpu.VMEM((4, 2, 192, 128), F32),
            pltpu.VMEM((2, 2, RP * 8, 128), F32),
            pltpu.VMEM((2, RP * 16, 256), BF),
        ],
        compiler_params=pltpu.CompilerParams(vmem_limit_bytes=56 * 2**20),
        name="denoise",
    )(edge, movie, halo, mats, lift_mats, lift_weight, lift_bias, out_weight)


def relay_kernel(foot_any, after_ref, out_any, in_ref, s_ref, o_ref, in_sem, out_sem):
    slots = foot_any.shape[0]
    parts = R // 16
    pitch = slots + 8

    def load(g):
        return pltpu.make_async_copy(
            foot_any.at[:, pl.ds(16 * g, 16), :], in_ref.at[g % 2], in_sem.at[g % 2]
        )

    def save(g):
        return pltpu.make_async_copy(
            o_ref.at[g % 2], out_any.at[pl.ds(8 * g, 8)], out_sem.at[g % 2]
        )

    load(0).start()

    for g in range(parts):
        if g + 1 < parts:
            load(g + 1).start()
        load(g).wait()

        def slot(b, _):
            for u in range(16):
                s = b * 16 + u
                s_ref[pl.ds(s, 16, stride=pitch), :] = in_ref[g % 2, s].astype(F32)
            return 0

        lax.fori_loop(0, slots // 16, slot, 0)
        if g >= 2:
            save(g - 2).wait()
        for q in range(8):
            two = [s_ref[(2 * q + e) * pitch : (2 * q + e) * pitch + slots, :] for e in range(2)]
            o_ref[g % 2, q] = jnp.concatenate(two, axis=1).astype(BF)
        save(g).start()
    for g in range(parts - 2, parts):
        save(g).wait()


def relay(footprints, after):
    slots = footprints.shape[0]
    return pl.pallas_call(
        relay_kernel,
        out_shape=jax.ShapeDtypeStruct((R // 2, slots, 256), BF),
        in_specs=[HBM, VMEM],
        out_specs=HBM,
        scratch_shapes=[
            pltpu.VMEM((2, slots, 16, 128), BF),
            pltpu.VMEM((16 * (slots + 8), 128), F32),
            pltpu.VMEM((2, 8, slots, 256), BF),
            pltpu.SemaphoreType.DMA((2,)),
            pltpu.SemaphoreType.DMA((2,)),
        ],
        compiler_params=pltpu.CompilerParams(vmem_limit_bytes=61 * 2**20),
        cost_estimate=pl.CostEstimate(flops=20_000_000, bytes_accessed=12_000_000, transcendentals=0),
        name="relay",
    )(footprints, after)


def trace_kernel(
    got_ref, tk_ref, foot_any, own_ref, id_ref, filt_ref, send_ref, g_ref, foot_ref, sem
):
    half = 4
    pitch = NT + 8
    parts = R // 16
    copies = [
        pltpu.make_async_copy(
            foot_any.at[pl.ds(8 * g, 8)], foot_ref.at[pl.ds(8 * g, 8)], sem.at[g]
        )
        for g in range(parts)
    ]
    for copy in copies:
        copy.start()
    traces = jnp.zeros((foot_ref.shape[1], NT), F32)
    for g in range(parts):
        r0 = 16 * g
        frames = [got_ref[t, r0 : r0 + 16, :].astype(F32) for t in range(NT)]
        for t in range(NT):
            total = None
            for k in range(2 * half + 1):
                u = t + k - half
                if 0 <= u < NT:
                    term = tk_ref[k] * frames[u]
                    total = term if total is None else total + term
            out = total.astype(BF)
            filt_ref[t, r0 : r0 + 16, :] = out
            g_ref[pl.ds(t, 16, stride=pitch), :] = out.astype(F32)
        copies[g].wait()
        for q in range(8):
            two = [g_ref[(2 * q + e) * pitch : (2 * q + e) * pitch + NT, :] for e in range(2)]
            rows = jnp.concatenate(two, axis=1).astype(BF)
            traces = traces + lax.dot_general(
                foot_ref[8 * g + q], rows, (((1,), (1,)), ((), ())), preferred_element_type=F32
            )
    slots = foot_any.shape[1]
    own_row = own_ref[...]
    r_of = lax.broadcasted_iota(jnp.int32, (slots, slots), 0)
    c_of = lax.broadcasted_iota(jnp.int32, (slots, slots), 1)

    def column(row):
        picked = jnp.where(r_of == c_of, row.astype(F32), 0.0)
        return jnp.sum(picked, axis=1, keepdims=True).astype(jnp.int32)

    own_col = column(own_row)
    rank = jnp.where((own_row == own_col) & (r_of < c_of), 1.0, 0.0)
    rank = jnp.sum(rank, axis=0, keepdims=True).astype(jnp.int32)
    place = own_row * CAP + rank
    hot = place == lax.broadcasted_iota(jnp.int32, (send_ref.shape[0], slots), 0)
    hot = hot.astype(F32).astype(BF)
    ids = column(id_ref[...])
    second = lax.broadcasted_iota(jnp.int32, (slots, 2), 1) == 1
    ids = jnp.where(second, ids % ID_BASE, ids // ID_BASE).astype(F32)
    sending = jnp.concatenate([traces, ids], axis=1)
    send_ref[...] = jnp.dot(
        hot, sending.astype(BF), preferred_element_type=F32
    ).astype(BF)


def trace(received, temporal_kernel, foot, slot_owner, slot_neuron, n_dev):
    slots = foot.shape[1]
    return pl.pallas_call(
        trace_kernel,
        out_shape=(
            jax.ShapeDtypeStruct((NT, R, 128), BF),
            jax.ShapeDtypeStruct((n_dev * CAP, NT + 2), BF),
        ),
        in_specs=[VMEM, SMEM, HBM, VMEM, VMEM],
        out_specs=(VMEM, VMEM),
        scratch_shapes=[
            pltpu.VMEM((16 * (NT + 8), 128), F32),
            pltpu.VMEM(foot.shape, BF),
            pltpu.SemaphoreType.DMA((R // 16,)),
        ],
        compiler_params=pltpu.CompilerParams(vmem_limit_bytes=50 * 2**20),
        name="trace",
    )(received, temporal_kernel, foot, slot_owner.reshape(1, slots), slot_neuron.reshape(1, slots))


def gather_kernel(got_ref, out_ref):
    got = got_ref[...].astype(F32)
    ids = got[:, NT : NT + 1] * ID_BASE + got[:, NT + 1 : NT + 2]
    n_of = lax.broadcasted_iota(jnp.int32, (got.shape[0], NEUR_DEV), 1)
    hot = (n_of == ids.astype(jnp.int32)).astype(F32).astype(BF)
    out_ref[...] = lax.dot_general(
        got_ref[:, :NT], hot, (((0,), (0,)), ((), ())), preferred_element_type=F32
    )


def gather(got):
    return pl.pallas_call(
        gather_kernel,
        out_shape=jax.ShapeDtypeStruct((NT, NEUR_DEV), F32),
        in_specs=[VMEM],
        out_specs=VMEM,
        name="gather",
    )(got).T


def local(
    movie,
    lift_weight,
    lift_bias,
    depth_kernel,
    mix_weight,
    mix_bias,
    out_weight,
    temporal_kernel,
    footprints,
    slot_owner,
    slot_neuron,
):
    n_tile = lax.axis_size("tile")
    me = lax.axis_index("tile")
    up = [(i, i + 1) for i in range(n_tile - 1)]
    down = [(b, a) for a, b in up]
    low = lax.ppermute(movie[:, R - HALO :], "tile", up)
    high = lax.ppermute(movie[:, :HALO], "tile", down)
    halo = jnp.concatenate([low, high], axis=1).reshape(2, 4 * HALO, W)
    halo = jnp.pad(halo, ((0, 0), (0, 16 - 4 * HALO), (0, 0)))
    edge = jnp.stack([me == 0, me == n_tile - 1]).astype(jnp.int32)
    mats, lift_mats = mix_matrices(depth_kernel, mix_weight, mix_bias, lift_weight, lift_bias)
    denoised, after = denoise(
        edge, movie.reshape(2, 2 * R, W), halo, mats, lift_mats, lift_weight, lift_bias, out_weight
    )
    n_dev = lax.axis_size("tm") * n_tile
    received = lax.all_to_all(denoised, "tm", 0, 0, tiled=True)
    foot = relay(footprints, after)
    filtered, outgoing = trace(
        received.reshape(NT, R, 128), temporal_kernel, foot, slot_owner, slot_neuron, n_dev
    )
    arriving = lax.all_to_all(
        outgoing.reshape(n_dev, CAP, NT + 2), ("tm", "tile"), 0, 0, tiled=True
    )
    return filtered, gather(arriving.reshape(n_dev * CAP, NT + 2))


def solution(mesh):
    return jax.shard_map(
        local,
        mesh=mesh,
        in_specs=(
            P("tm", "tile", None),
            P(),
            P(),
            P(),
            P(),
            P(),
            P(),
            P(),
            P(None, "tile", "tm"),
            P(("tm", "tile"), None),
            P(("tm", "tile")),
        ),
        out_specs=(P(None, "tile", "tm"), P(("tm", "tile"), None)),
        check_vma=False,
    )
```
